512 devices in a mesh: dp: 64 (over x, z_lo, core), mp: 8 (over y, z_hi).
Axes of the slice: x: 4, y: 4, z: 16 (z_hi: 2, z_lo: 8; z = z_hi * 8 + z_lo), core: 2. Of those that a mesh axis runs over, the one named last changes fastest.
Arguments:
- states: bfloat16 [128, 64, 2048], P('dp', None, 'mp'), may hold values from -6 to 6
- w_qkv: bfloat16 [3, 2048, 2048], P(None, 'dp', 'mp'), may hold values from -0.125 to 0.125
- w_out: bfloat16 [2048, 2048], P('dp', 'mp'), may hold values from -0.125 to 0.125
- cache_keys: bfloat16 [128, 384, 2048], P('dp', None, 'mp'), as said below
- cache_values: bfloat16 [128, 384, 2048], P('dp', None, 'mp'), may hold values from -6 to 6
- parents: int32 [128, 64], P('dp'), may hold values from 0 to 62, as said below
- accept: int32 [128, 8], P('dp'), may hold values from 0 to 63, as said below
- lengths: int32 [128], replicated, may hold values from 48 to 384
- perm: int32 [128], replicated, may hold values from 0 to 127, each once
Outputs:
- tree_out: bfloat16 [128, 64, 2048], P('dp', None, 'mp')
- new_keys: bfloat16 [128, 8, 2048], P('dp', None, 'mp')
- new_values: bfloat16 [128, 8, 2048], P('dp', None, 'mp')
The draws below stay inside these ranges and needn't reach their ends.
Inputs may be any that keep to these rules, and one draw needn't show every extreme that they name: parents[r, 0] = 0 for the root and parents[r, i] < i for every other node. `accept`: each row is a chain of 8 nodes from the root (node 0) downward, each entry the parent of the next. `perm`: each request stands in exactly one slot. `cache_keys`: keys of earlier positions, already rotated; slots at or past the request's length hold arbitrary values.
All inputs are finite; a program needn't handle non-finite values.
Results may differ from the reference program's by a relative error of at most 0.012.
The reference program's roundings to bfloat16 on the way count: a program that leaves them out, or rounds other values in their place, can miss the bound.
Values may be sent and summed in bfloat16 or wider, within the bound.
A program may use at most 64 MiB of HBM per device.

```python
import jax
import jax.numpy as jnp
from jax import lax

D = 2048
HEADS = 16
HEAD_DIM = 128
R_DEV = 2
TREE = 64
DEPTH = 8
CACHE = 384
REQS = 128


def draw_cache_keys(key, part):
    base = jax.random.normal(jax.random.fold_in(key, 11), (REQS, CACHE, D), jnp.float32)
    return base.astype(jnp.bfloat16)


def draw_lengths(key, part):
    base = jax.random.randint(jax.random.fold_in(key, 21), (REQS,), CACHE // 8, CACHE + 1)
    order = jax.random.permutation(jax.random.fold_in(key, 22), REQS)
    base = base.at[order[0]].set(CACHE)
    base = base.at[order[1]].set(CACHE // 8)
    return base.astype(jnp.int32)


def tree_draw(key):
    seed_key = jax.random.fold_in(key, 31)
    line_every = max(R_DEV, 2)

    def one_tree(request):
        sub_key = jax.random.fold_in(seed_key, request)
        chosen = jax.random.permutation(jax.random.fold_in(sub_key, 1), TREE - 3)[:DEPTH - 3] + 1
        tail = jnp.array([TREE - 2, TREE - 1], dtype=jnp.int32)
        chain = jnp.concatenate([jnp.zeros((1,), jnp.int32), jnp.sort(chosen).astype(jnp.int32), tail])
        raw_ids = jax.random.randint(jax.random.fold_in(sub_key, 2), (TREE,), 0, 1 << 20)
        node_ids = jnp.arange(TREE, dtype=jnp.int32)
        parent_ids = raw_ids % jnp.maximum(node_ids, 1)
        parent_ids = parent_ids.at[chain[1:]].set(chain[:-1])
        straight = request % line_every == 0
        line_parents = jnp.maximum(node_ids - 1, 0)
        line_chain = jnp.arange(DEPTH, dtype=jnp.int32)
        parent_ids = jnp.where(straight, line_parents, parent_ids)
        chain = jnp.where(straight, line_chain, chain)
        return (parent_ids.astype(jnp.int32), chain.astype(jnp.int32))
    return jax.vmap(one_tree)(jnp.arange(REQS, dtype=jnp.int32))


def draw_parents(key, part):
    return tree_draw(key)[0]


def draw_accept(key, part):
    return tree_draw(key)[1]


def levels(key, extent, cuts, least, high):
    level, own = 1.0, jax.random.fold_in(key, 6)
    for dim, shards_of in cuts:
        draws = jnp.exp(jax.random.uniform(jax.random.fold_in(own, dim), (shards_of,), jnp.float32, least / len(cuts), high / len(cuts)))
        level = level * jnp.repeat(draws, extent[dim] // shards_of).reshape([-1 if axis == dim else 1 for axis in range(len(extent))])
    return level


def normal_values(stream_key, dims, width, most, shards=(), held_as=jnp.bfloat16):
    values = width * jax.random.normal(stream_key, dims, jnp.float32)
    if shards:
        values = values * levels(stream_key, dims, shards, -0.22, 0.18)
    return jnp.clip(values, -most, most).astype(held_as)


def setup_inputs(seed: int = 0) -> dict:
    key_list = jax.random.split(jax.random.key(seed), 10)
    states = normal_values(key_list[0], (REQS, TREE, D), 1.0, 6.0, ((0, 64), (2, 8)))
    w_qkv = normal_values(key_list[1], (3, D, D), D ** -0.5, 0.125, ((1, 64), (2, 8)))
    w_out = normal_values(key_list[2], (D, D), D ** -0.5, 0.125, ((0, 64), (1, 8)))
    cache_keys = draw_cache_keys(jax.random.fold_in(key_list[9], 71), 0)
    cache_values = normal_values(key_list[4], (REQS, CACHE, D), 1.0, 6.0, ((0, 64), (2, 8)))
    parents = draw_parents(jax.random.fold_in(key_list[9], 71), 0)
    accept = draw_accept(jax.random.fold_in(key_list[9], 71), 0)
    lengths = draw_lengths(jax.random.fold_in(key_list[9], 71), 0)
    perm = jax.random.permutation(key_list[8], REQS).astype(jnp.int32)
    return {"states": states, "w_qkv": w_qkv, "w_out": w_out, "cache_keys": cache_keys, "cache_values": cache_values, "parents": parents, "accept": accept, "lengths": lengths, "perm": perm}


EPSILON = 1e-05
ROPE_BASE = 10000.0
NEG_FILL = -1e+30

def layer_norm(rows):
    mean_val = lax.optimization_barrier(jnp.mean(rows, axis=-1, keepdims=True))
    centred = rows - mean_val
    variance = lax.optimization_barrier(jnp.mean(centred * centred, axis=-1, keepdims=True))
    return centred * lax.rsqrt(variance + EPSILON)

def rotate(values, position):
    half = values.shape[-1] // 2
    freqs = ROPE_BASE ** (-(jnp.arange(half, dtype=jnp.float32) * 2.0 / values.shape[-1]))
    angle = position[:, :, None, None] * freqs
    cosine = jnp.cos(angle)
    sine = jnp.sin(angle)
    first = values[..., :half]
    second = values[..., half:]
    return jnp.concatenate([first * cosine - second * sine, second * cosine + first * sine], axis=-1)

def closure(parents):
    tree_len = parents.shape[-1]
    node_ids = jnp.arange(tree_len, dtype=jnp.int32)
    linked = (parents[:, :, None] == node_ids[None, None, :]) & (node_ids[None, :, None] > 0)
    reach = jnp.eye(tree_len, dtype=jnp.float32)[None] + linked.astype(jnp.float32)
    covered = 1
    while covered < tree_len:
        reach = jnp.minimum(jnp.einsum('rij,rjk->rik', reach, reach), 1.0)
        covered = covered * 2
    return reach

def attend(inputs):
    queries, keys_new, values_new, keys_old, values_old, reach, own_len = inputs
    scale = HEAD_DIM ** (-0.5)
    cache_len = keys_old.shape[0]
    keys_old = keys_old.reshape(cache_len, HEADS, HEAD_DIM).astype(jnp.float32)
    values_old = values_old.reshape(cache_len, HEADS, HEAD_DIM).astype(jnp.float32)
    qf = queries.astype(jnp.float32)
    cache_scores = jnp.einsum('thd,chd->htc', qf, keys_old) * scale
    valid = jnp.arange(cache_len, dtype=jnp.int32) < own_len
    cache_scores = jnp.where(valid[None, None, :], cache_scores, NEG_FILL)
    tree_scores = jnp.einsum('thd,shd->hts', qf, keys_new.astype(jnp.float32)) * scale
    tree_scores = jnp.where(reach[None] > 0, tree_scores, NEG_FILL)
    peak = jnp.maximum(lax.optimization_barrier(jnp.max(cache_scores, axis=-1)), lax.optimization_barrier(jnp.max(tree_scores, axis=-1)))
    cache_exp = jnp.exp(cache_scores - peak[..., None])
    tree_exp = jnp.exp(tree_scores - peak[..., None])
    denom = lax.optimization_barrier(jnp.sum(cache_exp, axis=-1)) + lax.optimization_barrier(jnp.sum(tree_exp, axis=-1))
    cache_prob = (cache_exp / denom[..., None]).astype(jnp.bfloat16)
    tree_prob = (tree_exp / denom[..., None]).astype(jnp.bfloat16)
    mixed = jnp.einsum('htc,chd->thd', cache_prob.astype(jnp.float32), values_old)
    mixed = mixed + jnp.einsum('hts,shd->thd', tree_prob.astype(jnp.float32), values_new.astype(jnp.float32))
    return mixed.astype(jnp.bfloat16).reshape(mixed.shape[0], -1)

def reference(states, w_qkv, w_out, cache_keys, cache_values, parents, accept, lengths, perm):
    req_count = states.shape[0]
    tree_len = states.shape[1]
    normed = layer_norm(states.astype(jnp.float32)).astype(jnp.bfloat16).reshape(req_count * tree_len, D)
    projected = []
    for which in range(3):
        flat = jnp.dot(normed, w_qkv[which], preferred_element_type=jnp.float32)
        projected.append(flat.reshape(req_count, tree_len, HEADS, HEAD_DIM))
    reach = closure(parents)
    depth = lax.optimization_barrier(jnp.sum(reach, axis=-1)) - 1.0
    own_lengths = lengths[perm.astype(jnp.int32)].astype(jnp.int32)
    position = own_lengths.astype(jnp.float32)[:, None] + depth
    queries = rotate(projected[0], position).astype(jnp.bfloat16)
    keys_new = rotate(projected[1], position).astype(jnp.bfloat16)
    values_new = projected[2].astype(jnp.bfloat16)
    attended = lax.map(attend, (queries, keys_new, values_new, cache_keys, cache_values, reach, own_lengths))
    flat_out = jnp.dot(attended.reshape(req_count * tree_len, D), w_out, preferred_element_type=jnp.float32)
    tree_out = (states.astype(jnp.float32) + flat_out.reshape(req_count, tree_len, D)).astype(jnp.bfloat16)
    index = accept.astype(jnp.int32)[:, :, None]
    new_keys = jnp.take_along_axis(keys_new.reshape(req_count, tree_len, D), index, axis=1)
    new_values = jnp.take_along_axis(values_new.reshape(req_count, tree_len, D), index, axis=1)
    return (tree_out, new_keys, new_values)
```

```python
import functools

import jax
import jax.numpy as jnp
import numpy as np
from jax import lax
from jax.experimental import pallas as pl
from jax.experimental.pallas import tpu as pltpu
from jax.sharding import PartitionSpec as P

HEAD_DIM = 128
EPSILON = 1e-05
ROPE_BASE = 10000.0
NEG_FILL = -1e30
MESH = pl.DeviceIdType.MESH
F32 = jnp.float32
BF16 = jnp.bfloat16


def mod4(value):
    return lax.rem(value + 8, 4)


class Links:
    def __init__(self):
        self.started = []

    def send(self, view, send_sem, recv_sem, device):
        copy = pltpu.make_async_remote_copy(
            src_ref=view, dst_ref=view, send_sem=send_sem, recv_sem=recv_sem,
            device_id=device, device_id_type=MESH,
        )
        copy.start()
        self.started.append(copy)

    def arrive(self, view, send_sem, recv_sem, device):
        pltpu.make_async_remote_copy(
            src_ref=view, dst_ref=view, send_sem=send_sem, recv_sem=recv_sem,
            device_id=device, device_id_type=MESH,
        ).wait_recv()

    def drain(self):
        for copy in self.started:
            copy.wait_send()


class Gather:
    def __init__(self, links, place, shard, batch, zs, zr, xs, xr, cs, cr):
        self.links, self.place, self.shard, self.batch = links, place, shard, batch
        self.zs, self.zr, self.xs, self.xr, self.cs, self.cr = zs, zr, xs, xr, cs, cr

    def z_source(self, index):
        p = self.place
        group = p.g if index < 4 else 1 - p.g
        return group * 4 + mod4(p.q - index % 4)

    def x_source(self, step):
        return mod4(self.place.x - step)

    def view(self, index, step, core):
        return self.shard(self.x_source(step) * 8 + self.z_source(index), core)

    def to_group(self, base):
        p = self.place
        for k in (1, 2, 3):
            device = p.at(zl=p.g * 4 + mod4(p.q + k))
            self.links.send(self.view(base, 0, p.c), self.zs.at[base + k], self.zr.at[base + k], device)

    def to_other_group(self):
        p = self.place
        self.links.send(self.view(0, 0, p.c), self.zs.at[4], self.zr.at[4], p.at(zl=(1 - p.g) * 4 + p.q))

    def to_x_and_core(self, index):
        p = self.place
        for step in (1, 3, 2):
            self.links.send(
                self.view(index, 0, p.c), self.xs.at[index, step], self.xr.at[index, step], p.at(x=mod4(p.x + step))
            )
        self.links.send(self.view(index, 0, p.c), self.cs.at[index], self.cr.at[index], p.at(c=1 - p.c))

    def z_arrive(self, index):
        p = self.place
        self.links.arrive(self.view(index, 0, p.c), self.zs.at[index], self.zr.at[index], p.at(c=1 - p.c))

    def x_arrive(self, step, half):
        p = self.place
        for index in range(4 * half, 4 * half + 4):
            self.links.arrive(
                self.view(index, step, p.c), self.xs.at[index, step], self.xr.at[index, step], p.at(c=1 - p.c)
            )

    def group_view(self, step, half, core):
        group = self.place.g if half == 0 else 1 - self.place.g
        return self.batch(self.x_source(step) * 8 + group * 4, core)

    def x_to_core(self, step, half):
        p = self.place
        slot = 8 + (step - 1) * 2 + half
        self.links.send(self.group_view(step, half, p.c), self.cs.at[slot], self.cr.at[slot], p.at(c=1 - p.c))

    def core_arrive(self, step):
        p = self.place
        if step == 0:
            for index in range(8):
                self.links.arrive(self.view(index, 0, 1 - p.c), self.cs.at[index], self.cr.at[index], p.at(c=1 - p.c))
        else:
            for half in (0, 1):
                slot = 8 + (step - 1) * 2 + half
                self.links.arrive(
                    self.group_view(step, half, 1 - p.c), self.cs.at[slot], self.cr.at[slot], p.at(c=1 - p.c)
                )


class Heads:
    def __init__(self, links, place, piece, ss, rs):
        self.links, self.place, self.piece, self.ss, self.rs = links, place, piece, ss, rs

    def to_y(self, far):
        p = self.place
        slot = p.y * 2 + (1 - p.zh if far else p.zh)
        for step in (1, 3, 2):
            index = far * 4 + step
            self.links.send(self.piece(slot), self.ss.at[index], self.rs.at[index], p.at(y=mod4(p.y + step)))

    def to_far(self):
        p = self.place
        self.links.send(self.piece(p.y * 2 + p.zh), self.ss.at[0], self.rs.at[0], p.at(zh=1 - p.zh))

    def far_arrive(self):
        p = self.place
        self.links.arrive(self.piece(p.y * 2 + 1 - p.zh), self.ss.at[0], self.rs.at[0], p.at(zh=1 - p.zh))

    def y_arrive(self, far):
        p = self.place
        for step in (1, 3, 2):
            index = far * 4 + step
            slot = mod4(p.y - step) * 2 + (1 - p.zh if far else p.zh)
            self.links.arrive(self.piece(slot), self.ss.at[index], self.rs.at[index], p.at(c=1 - p.c))


class Place:
    def __init__(self):
        dp, mp = lax.axis_index("dp"), lax.axis_index("mp")
        self.dp, self.mp = dp, mp
        self.x, self.zl, self.c = lax.div(dp, 16), lax.rem(lax.div(dp, 2), 8), lax.rem(dp, 2)
        self.g, self.q = lax.div(self.zl, 4), lax.rem(self.zl, 4)
        self.y, self.zh = lax.div(mp, 2), lax.rem(mp, 2)

    def at(self, x=None, zl=None, c=None, y=None, zh=None):
        x = self.x if x is None else x
        zl = self.zl if zl is None else zl
        c = self.c if c is None else c
        y = self.y if y is None else y
        zh = self.zh if zh is None else zh
        return (x * 16 + zl * 2 + c, y * 2 + zh)

    def peers(self):
        found = [self.at(c=1 - self.c)]
        found += [self.at(x=mod4(self.x + k)) for k in (1, 2, 3)]
        found += [self.at(y=mod4(self.y + k)) for k in (1, 2, 3)]
        found += [self.at(zl=self.g * 4 + mod4(self.q + k)) for k in (1, 2, 3)]
        found += [self.at(zl=(1 - self.g) * 4 + self.q), self.at(zh=1 - self.zh)]
        return found


def kernel(
    states_hbm, wqkv_hbm, wout_hbm, ck_hbm, cv_hbm, parents_ref, accept_ref, lengths_ref, perm_ref, freq_ref,
    out_ref, nk_ref, nv_ref,
    wbuf, obuf_w, sbuf, hbuf, abuf, kc, vc, acc, reach_ref, cos_ref, sin_ref, qb, kb, vb,
    loc, zs0, zr0, xs0, xr0, cs0, cr0, zs1, zr1, xs1, xr1, cs1, cr1, ss, rs, as0, ar0, as1, ar1,
):
    p = Place()
    links = Links()
    slot_own = p.x * 8 + p.zl
    local = [
        pltpu.make_async_copy(wqkv_hbm, wbuf.at[:, slot_own, p.c], loc.at[0]),
        pltpu.make_async_copy(states_hbm, sbuf.at[p.mp], loc.at[1]),
        pltpu.make_async_copy(wout_hbm, obuf_w.at[slot_own, p.c], loc.at[2]),
        pltpu.make_async_copy(ck_hbm, kc, loc.at[3]),
        pltpu.make_async_copy(cv_hbm, vc, loc.at[4]),
    ]
    for copy in local:
        copy.start()
    barrier = pltpu.get_barrier_semaphore()
    peers = p.peers()
    for device in peers:
        pl.semaphore_signal(barrier, inc=1, device_id=device, device_id_type=MESH)

    qkv = Gather(
        links, p, lambda slot, core: wbuf.at[:, slot, core],
        lambda slot, core: wbuf.at[:, pl.ds(slot, 4), core], zs0, zr0, xs0, xr0, cs0, cr0,
    )
    proj = Gather(
        links, p, lambda slot, core: obuf_w.at[slot, core],
        lambda slot, core: obuf_w.at[pl.ds(slot, 4), core], zs1, zr1, xs1, xr1, cs1, cr1,
    )
    rows = Heads(links, p, lambda slot: sbuf.at[slot], ss, rs)
    mixed = [
        Heads(links, p, lambda slot: abuf.at[slot, 0], as0, ar0),
        Heads(links, p, lambda slot: abuf.at[slot, 1], as1, ar1),
    ]

    local[0].wait()
    local[1].wait()
    local[2].wait()
    pl.semaphore_wait(barrier, len(peers))

    rows.to_far()
    qkv.to_other_group()
    qkv.to_group(0)
    qkv.to_x_and_core(0)
    rows.to_y(0)

    tree = 64
    row_id = lax.broadcasted_iota(jnp.int32, (tree, tree), 0)
    col_id = lax.broadcasted_iota(jnp.int32, (tree, tree), 1)
    col_f = col_id.astype(F32)
    own_len = []
    for r in range(2):
        own_len.append(lengths_ref[perm_ref[p.dp * 2 + r]])
        line = parents_ref[r : r + 1, :].astype(F32)
        column = jnp.sum(jnp.where(row_id == col_id, line, 0.0), axis=1, keepdims=True)
        linked = jnp.where((column == col_f) & (row_id > 0), 1.0, 0.0)
        reach = jnp.where(row_id == col_id, 1.0, 0.0) + linked
        for _ in range(6):
            half = reach.astype(BF16)
            reach = jnp.minimum(jnp.dot(half, half, preferred_element_type=F32), 1.0)
        reach_ref[r] = reach
        depth = jnp.sum(reach, axis=1, keepdims=True) - 1.0
        position = own_len[r].astype(F32) + depth
        angle = position * freq_ref[...]
        lane = lax.broadcasted_iota(jnp.int32, (tree, HEAD_DIM), 1)
        sine = jnp.sin(angle)
        cos_ref[r] = jnp.cos(angle)
        sin_ref[r] = jnp.where(lane < HEAD_DIM // 2, -sine, sine)

    for index in (1, 2, 3):
        qkv.z_arrive(index)
        qkv.to_x_and_core(index)
    qkv.z_arrive(4)
    qkv.to_group(4)
    qkv.to_x_and_core(4)
    rows.far_arrive()
    rows.to_y(1)
    proj.to_other_group()
    proj.to_group(0)
    for index in (5, 6, 7):
        qkv.z_arrive(index)
        qkv.to_x_and_core(index)
    for half in (0, 1):
        for step in (1, 3, 2):
            qkv.x_arrive(step, half)
            qkv.x_to_core(step, half)

    rows.y_arrive(0)
    rows.y_arrive(1)
    flat, width = 128, 256
    total = jnp.zeros((flat, 1), F32)
    for m in range(8):
        total = total + jnp.sum(sbuf[m].reshape(flat, width).astype(F32), axis=1, keepdims=True)
    mean = total / 2048.0
    total = jnp.zeros((flat, 1), F32)
    for m in range(8):
        centred = sbuf[m].reshape(flat, width).astype(F32) - mean
        total = total + jnp.sum(centred * centred, axis=1, keepdims=True)
    inverse = lax.rsqrt(total / 2048.0 + EPSILON)
    for m in range(8):
        centred = sbuf[m].reshape(flat, width).astype(F32) - mean
        hbuf[:, m * width : (m + 1) * width] = (centred * inverse).astype(BF16)

    for step in (0, 1, 3, 2):
        qkv.core_arrive(step)
        xx = mod4(p.x - step)
        part = hbuf[:, pl.ds(pl.multiple_of(xx * 512, 512), 512)]
        for j in range(3):
            block = wbuf[j, pl.ds(xx * 8, 8)].reshape(512, width)
            product = jnp.dot(part, block, preferred_element_type=F32)
            if step == 0:
                acc[j] = product
            else:
                acc[j] = acc[j] + product

    proj.to_x_and_core(0)
    for index in (1, 2, 3):
        proj.z_arrive(index)
        proj.to_x_and_core(index)
    proj.z_arrive(4)
    proj.to_group(4)
    proj.to_x_and_core(4)

    local[3].wait()
    local[4].wait()
    scale = HEAD_DIM ** (-0.5)
    slots = lax.broadcasted_iota(jnp.int32, (tree, 384), 1)
    across = (((1,), (1,)), ((), ()))
    for head in range(2):
        lanes = slice(head * HEAD_DIM, (head + 1) * HEAD_DIM)
        for r in range(2):
            span = slice(r * tree, (r + 1) * tree)
            cosine, sine = cos_ref[r], sin_ref[r]

            def turned(j):
                value = acc[j, span, lanes]
                return (value * cosine + pltpu.roll(value, HEAD_DIM // 2, 1) * sine).astype(BF16)

            queries, keys, values = turned(0), turned(1), acc[2, span, lanes].astype(BF16)
            kb[r, :, lanes] = keys
            vb[r, :, lanes] = values
            cache = lax.dot_general(queries, kc[r, :, lanes], across, preferred_element_type=F32) * scale
            cache = jnp.where(slots < own_len[r], cache, NEG_FILL)
            nodes = lax.dot_general(queries, keys, across, preferred_element_type=F32) * scale
            nodes = jnp.where(reach_ref[r] > 0, nodes, NEG_FILL)
            peak = jnp.maximum(jnp.max(cache, axis=1, keepdims=True), jnp.max(nodes, axis=1, keepdims=True))
            cache = jnp.exp(cache - peak)
            nodes = jnp.exp(nodes - peak)
            denom = jnp.sum(cache, axis=1, keepdims=True) + jnp.sum(nodes, axis=1, keepdims=True)
            cache = (cache / denom).astype(BF16)
            nodes = (nodes / denom).astype(BF16)
            blend = jnp.dot(cache, vc[r, :, lanes], preferred_element_type=F32)
            blend = blend + jnp.dot(nodes, values, preferred_element_type=F32)
            abuf[p.mp, head, span, :] = blend.astype(BF16)
        mixed[head].to_far()
        mixed[head].to_y(0)

    for index in (5, 6, 7):
        proj.z_arrive(index)
        proj.to_x_and_core(index)

    for r in range(2):
        line = accept_ref[r : r + 1, :].astype(F32)
        small_row = lax.broadcasted_iota(jnp.int32, (8, 8), 0)
        small_col = lax.broadcasted_iota(jnp.int32, (8, 8), 1)
        column = jnp.sum(jnp.where(small_row == small_col, line, 0.0), axis=1, keepdims=True)
        picker = jnp.where(column == lax.broadcasted_iota(jnp.int32, (8, tree), 1).astype(F32), 1.0, 0.0).astype(BF16)
        nk_ref[r] = jnp.dot(picker, kb[r], preferred_element_type=F32).astype(BF16)
        nv_ref[r] = jnp.dot(picker, vb[r], preferred_element_type=F32).astype(BF16)

    for half in (0, 1):
        for step in (1, 3, 2):
            proj.x_arrive(step, half)
            proj.x_to_core(step, half)
    for step in (0, 1, 3, 2):
        proj.core_arrive(step)
    for head in range(2):
        mixed[head].far_arrive()
        mixed[head].to_y(1)
    for far in (0, 1):
        for head in range(2):
            mixed[head].y_arrive(far)

    result = sbuf[p.mp].reshape(flat, width).astype(F32)
    product = jnp.zeros((flat, width), F32)
    for m in range(8):
        both = jnp.concatenate([abuf[m, 0], abuf[m, 1]], axis=1)
        block = obuf_w[4 * m : 4 * m + 4].reshape(256, width)
        product = product + jnp.dot(both, block, preferred_element_type=F32)
    out_ref[...] = (result + product).astype(BF16).reshape(2, tree, width)
    links.drain()


def local(states, w_qkv, w_out, cache_keys, cache_values, parents, accept, lengths, perm):
    half = HEAD_DIM // 2
    freqs = ROPE_BASE ** (-(np.arange(half, dtype=np.float32) * np.float32(2.0) / np.float32(HEAD_DIM)))
    freqs = np.concatenate([freqs, freqs]).astype(np.float32)[None, :]
    hbm = pl.BlockSpec(memory_space=pl.ANY)
    vmem = pl.BlockSpec(memory_space=pltpu.VMEM)
    smem = pl.BlockSpec(memory_space=pltpu.SMEM)
    dma = pltpu.SemaphoreType.DMA
    gather_sems = [dma((8,)), dma((8,)), dma((8, 4)), dma((8, 4)), dma((14,)), dma((14,))]
    return pl.pallas_call(
        kernel,
        name="sublayer",
        out_shape=(
            jax.ShapeDtypeStruct((2, 64, 256), BF16),
            jax.ShapeDtypeStruct((2, 8, 256), BF16),
            jax.ShapeDtypeStruct((2, 8, 256), BF16),
        ),
        in_specs=[hbm, hbm, hbm, hbm, hbm, vmem, vmem, smem, smem, vmem],
        out_specs=(vmem, vmem, vmem),
        scratch_shapes=[
            pltpu.VMEM((3, 32, 2, 32, 256), BF16),
            pltpu.VMEM((32, 2, 32, 256), BF16),
            pltpu.VMEM((8, 2, 64, 256), BF16),
            pltpu.VMEM((128, 2048), BF16),
            pltpu.VMEM((8, 2, 128, 128), BF16),
            pltpu.VMEM((2, 384, 256), BF16),
            pltpu.VMEM((2, 384, 256), BF16),
            pltpu.VMEM((3, 128, 256), F32),
            pltpu.VMEM((2, 64, 64), F32),
            pltpu.VMEM((2, 64, 128), F32),
            pltpu.VMEM((2, 64, 128), F32),
            pltpu.VMEM((2, 64, 256), BF16),
            pltpu.VMEM((2, 64, 256), BF16),
            pltpu.VMEM((2, 64, 256), BF16),
            dma((5,)), *gather_sems, *gather_sems,
            dma((8,)), dma((8,)), dma((8,)), dma((8,)), dma((8,)), dma((8,)),
        ],
        compiler_params=pltpu.CompilerParams(collective_id=0, has_side_effects=True),
    )(states, w_qkv, w_out, cache_keys, cache_values, parents, accept, lengths, perm, jnp.asarray(freqs))


def solution(mesh):
    in_specs = (
        P("dp", None, "mp"),
        P(None, "dp", "mp"),
        P("dp", "mp"),
        P("dp", None, "mp"),
        P("dp", None, "mp"),
        P("dp", None),
        P("dp", None),
        P(),
        P(),
    )
    out_specs = (P("dp", None, "mp"), P("dp", None, "mp"), P("dp", None, "mp"))
    return jax.shard_map(local, mesh=mesh, in_specs=in_specs, out_specs=out_specs, check_vma=False)
```

```python
import functools

import jax
import jax.numpy as jnp
import numpy as np
from jax import lax
from jax.experimental import pallas as pl
from jax.experimental.pallas import tpu as pltpu
from jax.sharding import PartitionSpec as P

HEAD_DIM = 128
EPSILON = 1e-05
ROPE_BASE = 10000.0
NEG_FILL = -1e30
MESH = pl.DeviceIdType.MESH
F32 = jnp.float32
BF16 = jnp.bfloat16


def mod4(value):
    return lax.rem(value + 8, 4)


class Links:
    def __init__(self):
        self.started = []

    def send(self, view, send_sem, recv_sem, device):
        copy = pltpu.make_async_remote_copy(
            src_ref=view, dst_ref=view, send_sem=send_sem, recv_sem=recv_sem,
            device_id=device, device_id_type=MESH,
        )
        copy.start()
        self.started.append(copy)

    def arrive(self, view, send_sem, recv_sem, device):
        pltpu.make_async_remote_copy(
            src_ref=view, dst_ref=view, send_sem=send_sem, recv_sem=recv_sem,
            device_id=device, device_id_type=MESH,
        ).wait_recv()

    def drain(self):
        for copy in self.started:
            copy.wait_send()


class Gather:
    def __init__(self, links, place, shard, batch, zs, zr, xs, xr, cs, cr):
        self.links, self.place, self.shard, self.batch = links, place, shard, batch
        self.zs, self.zr, self.xs, self.xr, self.cs, self.cr = zs, zr, xs, xr, cs, cr

    def z_source(self, index):
        p = self.place
        group = p.g if index < 4 else 1 - p.g
        return group * 4 + mod4(p.q - index % 4)

    def x_source(self, step):
        return mod4(self.place.x - step)

    def view(self, index, step, core):
        return self.shard(self.x_source(step) * 8 + self.z_source(index), core)

    def to_group(self, base):
        p = self.place
        for k in (1, 2, 3):
            device = p.at(zl=p.g * 4 + mod4(p.q + k))
            self.links.send(self.view(base, 0, p.c), self.zs.at[base + k], self.zr.at[base + k], device)

    def to_other_group(self):
        p = self.place
        self.links.send(self.view(0, 0, p.c), self.zs.at[4], self.zr.at[4], p.at(zl=(1 - p.g) * 4 + p.q))

    def to_x_and_core(self, index):
        p = self.place
        for step in (1, 3, 2):
            self.links.send(
                self.view(index, 0, p.c), self.xs.at[index, step], self.xr.at[index, step], p.at(x=mod4(p.x + step))
            )
        self.links.send(self.view(index, 0, p.c), self.cs.at[index], self.cr.at[index], p.at(c=1 - p.c))

    def z_arrive(self, index):
        p = self.place
        self.links.arrive(self.view(index, 0, p.c), self.zs.at[index], self.zr.at[index], p.at(c=1 - p.c))

    def x_arrive(self, step, half):
        p = self.place
        for index in range(4 * half, 4 * half + 4):
            self.links.arrive(
                self.view(index, step, p.c), self.xs.at[index, step], self.xr.at[index, step], p.at(c=1 - p.c)
            )

    def group_view(self, step, half, core):
        group = self.place.g if half == 0 else 1 - self.place.g
        return self.batch(self.x_source(step) * 8 + group * 4, core)

    def x_to_core(self, step, half):
        p = self.place
        slot = 8 + (step - 1) * 2 + half
        self.links.send(self.group_view(step, half, p.c), self.cs.at[slot], self.cr.at[slot], p.at(c=1 - p.c))

    def core_arrive(self, step):
        p = self.place
        if step == 0:
            for index in range(8):
                self.links.arrive(self.view(index, 0, 1 - p.c), self.cs.at[index], self.cr.at[index], p.at(c=1 - p.c))
        else:
            for half in (0, 1):
                slot = 8 + (step - 1) * 2 + half
                self.links.arrive(
                    self.group_view(step, half, 1 - p.c), self.cs.at[slot], self.cr.at[slot], p.at(c=1 - p.c)
                )


class Heads:
    def __init__(self, links, place, piece, ss, rs):
        self.links, self.place, self.piece, self.ss, self.rs = links, place, piece, ss, rs

    def to_y(self, far):
        p = self.place
        slot = p.y * 2 + (1 - p.zh if far else p.zh)
        for step in (1, 3, 2):
            index = far * 4 + step
            self.links.send(self.piece(slot), self.ss.at[index], self.rs.at[index], p.at(y=mod4(p.y + step)))

    def to_far(self):
        p = self.place
        self.links.send(self.piece(p.y * 2 + p.zh), self.ss.at[0], self.rs.at[0], p.at(zh=1 - p.zh))

    def far_arrive(self):
        p = self.place
        self.links.arrive(self.piece(p.y * 2 + 1 - p.zh), self.ss.at[0], self.rs.at[0], p.at(zh=1 - p.zh))

    def y_arrive(self, far):
        p = self.place
        for step in (1, 3, 2):
            index = far * 4 + step
            slot = mod4(p.y - step) * 2 + (1 - p.zh if far else p.zh)
            self.links.arrive(self.piece(slot), self.ss.at[index], self.rs.at[index], p.at(c=1 - p.c))


class Place:
    def __init__(self):
        dp, mp = lax.axis_index("dp"), lax.axis_index("mp")
        self.dp, self.mp = dp, mp
        self.x, self.zl, self.c = lax.div(dp, 16), lax.rem(lax.div(dp, 2), 8), lax.rem(dp, 2)
        self.g, self.q = lax.div(self.zl, 4), lax.rem(self.zl, 4)
        self.y, self.zh = lax.div(mp, 2), lax.rem(mp, 2)

    def at(self, x=None, zl=None, c=None, y=None, zh=None):
        x = self.x if x is None else x
        zl = self.zl if zl is None else zl
        c = self.c if c is None else c
        y = self.y if y is None else y
        zh = self.zh if zh is None else zh
        return (x * 16 + zl * 2 + c, y * 2 + zh)

    def middle(self):
        return self.at(zl=(1 - self.g) * 4 + self.q, zh=1 - self.zh)

    def peers(self):
        found = [self.at(c=1 - self.c)]
        found += [self.at(x=mod4(self.x + k)) for k in (1, 2, 3)]
        found += [self.at(y=mod4(self.y + k)) for k in (1, 2, 3)]
        found += [self.at(zl=self.g * 4 + mod4(self.q + k)) for k in (1, 2, 3)]
        found += [self.at(zl=(1 - self.g) * 4 + self.q), self.middle()]
        return found


def kernel(
    states_hbm, wqkv_hbm, wout_hbm, ck_hbm, cv_hbm, parents_ref, accept_ref, lengths_ref, perm_ref, freq_ref,
    out_ref, nk_ref, nv_ref,
    wbuf, obuf_w, sbuf, hbuf, abuf, kc, vc, acc, reach_ref, cos_ref, sin_ref, qb, kb, vb,
    loc, zs0, zr0, xs0, xr0, cs0, cr0, zs1, zr1, xs1, xr1, cs1, cr1, ss, rs, as0, ar0, as1, ar1, far_ok,
):
    p = Place()
    links = Links()
    slot_own = p.x * 8 + p.zl
    local = [
        pltpu.make_async_copy(wqkv_hbm, wbuf.at[:, slot_own, p.c], loc.at[0]),
        pltpu.make_async_copy(states_hbm, sbuf.at[p.mp], loc.at[1]),
        pltpu.make_async_copy(wout_hbm, obuf_w.at[slot_own, p.c], loc.at[2]),
        pltpu.make_async_copy(ck_hbm, kc, loc.at[3]),
        pltpu.make_async_copy(cv_hbm, vc, loc.at[4]),
    ]
    for copy in local:
        copy.start()
    barrier = pltpu.get_barrier_semaphore()
    peers = p.peers()
    for device in peers:
        pl.semaphore_signal(barrier, inc=1, device_id=device, device_id_type=MESH)

    qkv = Gather(
        links, p, lambda slot, core: wbuf.at[:, slot, core],
        lambda slot, core: wbuf.at[:, pl.ds(slot, 4), core], zs0, zr0, xs0, xr0, cs0, cr0,
    )
    proj = Gather(
        links, p, lambda slot, core: obuf_w.at[slot, core],
        lambda slot, core: obuf_w.at[pl.ds(slot, 4), core], zs1, zr1, xs1, xr1, cs1, cr1,
    )
    rows = Heads(links, p, lambda slot: sbuf.at[slot], ss, rs)
    mixed = [
        Heads(links, p, lambda slot: abuf.at[slot, 0], as0, ar0),
        Heads(links, p, lambda slot: abuf.at[slot, 1], as1, ar1),
    ]

    local[0].wait()
    pl.semaphore_wait(barrier, len(peers))
    pl.semaphore_signal(far_ok, inc=1, device_id=p.middle(), device_id_type=MESH)

    qkv.to_other_group()
    qkv.to_group(0)
    qkv.to_x_and_core(0)
    local[1].wait()
    rows.to_y(0)

    tree = 64
    row_id = lax.broadcasted_iota(jnp.int32, (tree, tree), 0)
    col_id = lax.broadcasted_iota(jnp.int32, (tree, tree), 1)
    col_f = col_id.astype(F32)
    own_len = []
    for r in range(2):
        own_len.append(lengths_ref[perm_ref[p.dp * 2 + r]])
        line = parents_ref[r : r + 1, :].astype(F32)
        column = jnp.sum(jnp.where(row_id == col_id, line, 0.0), axis=1, keepdims=True)
        linked = jnp.where((column == col_f) & (row_id > 0), 1.0, 0.0)
        reach = jnp.where(row_id == col_id, 1.0, 0.0) + linked
        for _ in range(6):
            half = reach.astype(BF16)
            reach = jnp.minimum(jnp.dot(half, half, preferred_element_type=F32), 1.0)
        reach_ref[r] = reach
        depth = jnp.sum(reach, axis=1, keepdims=True) - 1.0
        position = own_len[r].astype(F32) + depth
        angle = position * freq_ref[...]
        lane = lax.broadcasted_iota(jnp.int32, (tree, HEAD_DIM), 1)
        sine = jnp.sin(angle)
        cos_ref[r] = jnp.cos(angle)
        sin_ref[r] = jnp.where(lane < HEAD_DIM // 2, -sine, sine)

    for index in (1, 2, 3):
        qkv.z_arrive(index)
        qkv.to_x_and_core(index)
    qkv.z_arrive(4)
    qkv.to_group(4)
    qkv.to_x_and_core(4)
    for index in (5, 6, 7):
        qkv.z_arrive(index)
        qkv.to_x_and_core(index)
    pl.semaphore_wait(far_ok, 1)
    rows.to_far()
    local[2].wait()
    proj.to_other_group()
    proj.to_group(0)
    for step in (1, 3, 2):
        qkv.x_arrive(step, 0)
        qkv.x_to_core(step, 0)
    rows.far_arrive()
    rows.to_y(1)
    for index in (1, 2, 3):
        proj.z_arrive(index)
    proj.z_arrive(4)
    proj.to_group(4)
    for step in (1, 3, 2):
        qkv.x_arrive(step, 1)
        qkv.x_to_core(step, 1)
    for index in (0, 1, 2, 3, 4):
        proj.to_x_and_core(index)

    rows.y_arrive(0)
    rows.y_arrive(1)
    flat, width = 128, 256
    total = jnp.zeros((flat, 1), F32)
    for m in range(8):
        total = total + jnp.sum(sbuf[m].reshape(flat, width).astype(F32), axis=1, keepdims=True)
    mean = total / 2048.0
    total = jnp.zeros((flat, 1), F32)
    for m in range(8):
        centred = sbuf[m].reshape(flat, width).astype(F32) - mean
        total = total + jnp.sum(centred * centred, axis=1, keepdims=True)
    inverse = lax.rsqrt(total / 2048.0 + EPSILON)
    for m in range(8):
        centred = sbuf[m].reshape(flat, width).astype(F32) - mean
        hbuf[:, m * width : (m + 1) * width] = (centred * inverse).astype(BF16)

    for index in (5, 6, 7):
        proj.z_arrive(index)
        proj.to_x_and_core(index)

    for step in (0, 1, 3, 2):
        qkv.core_arrive(step)
        xx = mod4(p.x - step)
        part = hbuf[:, pl.ds(pl.multiple_of(xx * 512, 512), 512)]
        for j in range(3):
            block = wbuf[j, pl.ds(xx * 8, 8)].reshape(512, width)
            product = jnp.dot(part, block, preferred_element_type=F32)
            if step == 0:
                acc[j] = product
            else:
                acc[j] = acc[j] + product

    local[3].wait()
    local[4].wait()
    scale = HEAD_DIM ** (-0.5)
    slots = lax.broadcasted_iota(jnp.int32, (tree, 384), 1)
    across = (((1,), (1,)), ((), ()))
    for head in range(2):
        lanes = slice(head * HEAD_DIM, (head + 1) * HEAD_DIM)
        for r in range(2):
            span = slice(r * tree, (r + 1) * tree)
            cosine, sine = cos_ref[r], sin_ref[r]

            def turned(j):
                value = acc[j, span, lanes]
                return (value * cosine + pltpu.roll(value, HEAD_DIM // 2, 1) * sine).astype(BF16)

            queries, keys, values = turned(0), turned(1), acc[2, span, lanes].astype(BF16)
            kb[r, :, lanes] = keys
            vb[r, :, lanes] = values
            cache = lax.dot_general(queries, kc[r, :, lanes], across, preferred_element_type=F32) * scale
            cache = jnp.where(slots < own_len[r], cache, NEG_FILL)
            nodes = lax.dot_general(queries, keys, across, preferred_element_type=F32) * scale
            nodes = jnp.where(reach_ref[r] > 0, nodes, NEG_FILL)
            peak = jnp.maximum(jnp.max(cache, axis=1, keepdims=True), jnp.max(nodes, axis=1, keepdims=True))
            cache = jnp.exp(cache - peak)
            nodes = jnp.exp(nodes - peak)
            denom = jnp.sum(cache, axis=1, keepdims=True) + jnp.sum(nodes, axis=1, keepdims=True)
            cache = (cache / denom).astype(BF16)
            nodes = (nodes / denom).astype(BF16)
            blend = jnp.dot(cache, vc[r, :, lanes], preferred_element_type=F32)
            blend = blend + jnp.dot(nodes, values, preferred_element_type=F32)
            abuf[p.mp, head, span, :] = blend.astype(BF16)
        mixed[head].to_far()
        mixed[head].to_y(0)

    for r in range(2):
        line = accept_ref[r : r + 1, :].astype(F32)
        small_row = lax.broadcasted_iota(jnp.int32, (8, 8), 0)
        small_col = lax.broadcasted_iota(jnp.int32, (8, 8), 1)
        column = jnp.sum(jnp.where(small_row == small_col, line, 0.0), axis=1, keepdims=True)
        picker = jnp.where(column == lax.broadcasted_iota(jnp.int32, (8, tree), 1).astype(F32), 1.0, 0.0).astype(BF16)
        nk_ref[r] = jnp.dot(picker, kb[r], preferred_element_type=F32).astype(BF16)
        nv_ref[r] = jnp.dot(picker, vb[r], preferred_element_type=F32).astype(BF16)

    for half in (0, 1):
        for step in (1, 3, 2):
            proj.x_arrive(step, half)
            proj.x_to_core(step, half)
    for step in (0, 1, 3, 2):
        proj.core_arrive(step)
    product = sbuf[p.mp].reshape(flat, width).astype(F32)

    def projected(m):
        both = jnp.concatenate([abuf[m, 0], abuf[m, 1]], axis=1)
        block = obuf_w[pl.ds(4 * m, 4)].reshape(256, width)
        return jnp.dot(both, block, preferred_element_type=F32)

    for head in range(2):
        mixed[head].y_arrive(0)
    for step in (0, 1, 3, 2):
        product = product + projected(mod4(p.y - step) * 2 + p.zh)
    for head in range(2):
        mixed[head].far_arrive()
        mixed[head].to_y(1)
    product = product + projected(p.y * 2 + 1 - p.zh)
    for head in range(2):
        mixed[head].y_arrive(1)
    for step in (1, 3, 2):
        product = product + projected(mod4(p.y - step) * 2 + 1 - p.zh)
    out_ref[...] = product.astype(BF16).reshape(2, tree, width)
    links.drain()


def local(states, w_qkv, w_out, cache_keys, cache_values, parents, accept, lengths, perm):
    half = HEAD_DIM // 2
    freqs = ROPE_BASE ** (-(np.arange(half, dtype=np.float32) * np.float32(2.0) / np.float32(HEAD_DIM)))
    freqs = np.concatenate([freqs, freqs]).astype(np.float32)[None, :]
    hbm = pl.BlockSpec(memory_space=pl.ANY)
    vmem = pl.BlockSpec(memory_space=pltpu.VMEM)
    smem = pl.BlockSpec(memory_space=pltpu.SMEM)
    dma = pltpu.SemaphoreType.DMA
    gather_sems = [dma((8,)), dma((8,)), dma((8, 4)), dma((8, 4)), dma((14,)), dma((14,))]
    return pl.pallas_call(
        kernel,
        name="sublayer",
        out_shape=(
            jax.ShapeDtypeStruct((2, 64, 256), BF16),
            jax.ShapeDtypeStruct((2, 8, 256), BF16),
            jax.ShapeDtypeStruct((2, 8, 256), BF16),
        ),
        in_specs=[hbm, hbm, hbm, hbm, hbm, vmem, vmem, smem, smem, vmem],
        out_specs=(vmem, vmem, vmem),
        scratch_shapes=[
            pltpu.VMEM((3, 32, 2, 32, 256), BF16),
            pltpu.VMEM((32, 2, 32, 256), BF16),
            pltpu.VMEM((8, 2, 64, 256), BF16),
            pltpu.VMEM((128, 2048), BF16),
            pltpu.VMEM((8, 2, 128, 128), BF16),
            pltpu.VMEM((2, 384, 256), BF16),
            pltpu.VMEM((2, 384, 256), BF16),
            pltpu.VMEM((3, 128, 256), F32),
            pltpu.VMEM((2, 64, 64), F32),
            pltpu.VMEM((2, 64, 128), F32),
            pltpu.VMEM((2, 64, 128), F32),
            pltpu.VMEM((2, 64, 256), BF16),
            pltpu.VMEM((2, 64, 256), BF16),
            pltpu.VMEM((2, 64, 256), BF16),
            dma((5,)), *gather_sems, *gather_sems,
            dma((8,)), dma((8,)), dma((8,)), dma((8,)), dma((8,)), dma((8,)), pltpu.SemaphoreType.REGULAR,
        ],
        compiler_params=pltpu.CompilerParams(collective_id=0, has_side_effects=True),
    )(states, w_qkv, w_out, cache_keys, cache_values, parents, accept, lengths, perm, jnp.asarray(freqs))


def solution(mesh):
    in_specs = (
        P("dp", None, "mp"),
        P(None, "dp", "mp"),
        P("dp", "mp"),
        P("dp", None, "mp"),
        P("dp", None, "mp"),
        P("dp", None),
        P("dp", None),
        P(),
        P(),
    )
    out_specs = (P("dp", None, "mp"), P("dp", None, "mp"), P("dp", None, "mp"))
    return jax.shard_map(local, mesh=mesh, in_specs=in_specs, out_specs=out_specs, check_vma=False)
```

```python
import functools

import jax
import jax.numpy as jnp
import numpy as np
from jax import lax
from jax.experimental import pallas as pl
from jax.experimental.pallas import tpu as pltpu
from jax.sharding import PartitionSpec as P

HEAD_DIM = 128
EPSILON = 1e-05
ROPE_BASE = 10000.0
NEG_FILL = -1e30
MESH = pl.DeviceIdType.MESH
F32 = jnp.float32
BF16 = jnp.bfloat16


def mod4(value):
    return lax.rem(value + 8, 4)


class Links:
    def __init__(self):
        self.started = []

    def send(self, view, send_sem, recv_sem, device):
        copy = pltpu.make_async_remote_copy(
            src_ref=view, dst_ref=view, send_sem=send_sem, recv_sem=recv_sem,
            device_id=device, device_id_type=MESH,
        )
        copy.start()
        self.started.append(copy)

    def arrive(self, view, send_sem, recv_sem, device):
        pltpu.make_async_remote_copy(
            src_ref=view, dst_ref=view, send_sem=send_sem, recv_sem=recv_sem,
            device_id=device, device_id_type=MESH,
        ).wait_recv()

    def drain(self):
        for copy in self.started:
            copy.wait_send()


class Gather:
    def __init__(self, links, place, shard, batch, zs, zr, xs, xr, cs, cr):
        self.links, self.place, self.shard, self.batch = links, place, shard, batch
        self.zs, self.zr, self.xs, self.xr, self.cs, self.cr = zs, zr, xs, xr, cs, cr

    def z_source(self, index):
        p = self.place
        group = p.g if index < 4 else 1 - p.g
        return group * 4 + mod4(p.q - index % 4)

    def x_source(self, step):
        return mod4(self.place.x - step)

    def view(self, index, step, core):
        return self.shard(self.x_source(step) * 8 + self.z_source(index), core)

    def to_group(self, base):
        p = self.place
        for k in (1, 2, 3):
            device = p.at(zl=p.g * 4 + mod4(p.q + k))
            self.links.send(self.view(base, 0, p.c), self.zs.at[base + k], self.zr.at[base + k], device)

    def to_other_group(self):
        p = self.place
        self.links.send(self.view(0, 0, p.c), self.zs.at[4], self.zr.at[4], p.at(zl=(1 - p.g) * 4 + p.q))

    def to_x_and_core(self, index):
        p = self.place
        for step in (1, 3, 2):
            self.links.send(
                self.view(index, 0, p.c), self.xs.at[index, step], self.xr.at[index, step], p.at(x=mod4(p.x + step))
            )
        self.links.send(self.view(index, 0, p.c), self.cs.at[index], self.cr.at[index], p.at(c=1 - p.c))

    def z_arrive(self, index):
        p = self.place
        self.links.arrive(self.view(index, 0, p.c), self.zs.at[index], self.zr.at[index], p.at(c=1 - p.c))

    def x_arrive(self, step, half):
        p = self.place
        for index in range(4 * half, 4 * half + 4):
            self.links.arrive(
                self.view(index, step, p.c), self.xs.at[index, step], self.xr.at[index, step], p.at(c=1 - p.c)
            )

    def group_view(self, step, half, core):
        group = self.place.g if half == 0 else 1 - self.place.g
        return self.batch(self.x_source(step) * 8 + group * 4, core)

    def x_to_core(self, step, half):
        p = self.place
        slot = 8 + (step - 1) * 2 + half
        self.links.send(self.group_view(step, half, p.c), self.cs.at[slot], self.cr.at[slot], p.at(c=1 - p.c))

    def core_arrive(self, step):
        p = self.place
        if step == 0:
            for index in range(8):
                self.links.arrive(self.view(index, 0, 1 - p.c), self.cs.at[index], self.cr.at[index], p.at(c=1 - p.c))
        else:
            for half in (0, 1):
                slot = 8 + (step - 1) * 2 + half
                self.links.arrive(
                    self.group_view(step, half, 1 - p.c), self.cs.at[slot], self.cr.at[slot], p.at(c=1 - p.c)
                )


class Heads:
    def __init__(self, links, place, piece, ss, rs):
        self.links, self.place, self.piece, self.ss, self.rs = links, place, piece, ss, rs

    def to_y(self, far):
        p = self.place
        slot = p.y * 2 + (1 - p.zh if far else p.zh)
        for step in (1, 3, 2):
            index = far * 4 + step
            self.links.send(self.piece(slot), self.ss.at[index], self.rs.at[index], p.at(y=mod4(p.y + step)))

    def to_far(self):
        p = self.place
        self.links.send(self.piece(p.y * 2 + p.zh), self.ss.at[0], self.rs.at[0], p.at(zh=1 - p.zh))

    def far_arrive(self):
        p = self.place
        self.links.arrive(self.piece(p.y * 2 + 1 - p.zh), self.ss.at[0], self.rs.at[0], p.at(zh=1 - p.zh))

    def y_arrive(self, far):
        p = self.place
        for step in (1, 3, 2):
            index = far * 4 + step
            slot = mod4(p.y - step) * 2 + (1 - p.zh if far else p.zh)
            self.links.arrive(self.piece(slot), self.ss.at[index], self.rs.at[index], p.at(c=1 - p.c))


class Place:
    def __init__(self):
        dp, mp = lax.axis_index("dp"), lax.axis_index("mp")
        self.dp, self.mp = dp, mp
        self.x, self.zl, self.c = lax.div(dp, 16), lax.rem(lax.div(dp, 2), 8), lax.rem(dp, 2)
        self.g, self.q = lax.div(self.zl, 4), lax.rem(self.zl, 4)
        self.y, self.zh = lax.div(mp, 2), lax.rem(mp, 2)

    def at(self, x=None, zl=None, c=None, y=None, zh=None):
        x = self.x if x is None else x
        zl = self.zl if zl is None else zl
        c = self.c if c is None else c
        y = self.y if y is None else y
        zh = self.zh if zh is None else zh
        return (x * 16 + zl * 2 + c, y * 2 + zh)

    def middle(self):
        return self.at(zl=(1 - self.g) * 4 + self.q, zh=1 - self.zh)

    def peers(self):
        found = [self.at(c=1 - self.c)]
        found += [self.at(x=mod4(self.x + k)) for k in (1, 2, 3)]
        found += [self.at(y=mod4(self.y + k)) for k in (1, 2, 3)]
        found += [self.at(zl=self.g * 4 + mod4(self.q + k)) for k in (1, 2, 3)]
        found += [self.at(zl=(1 - self.g) * 4 + self.q), self.middle()]
        return found


def kernel(
    states_hbm, wqkv_hbm, wout_hbm, ck_hbm, cv_hbm, parents_ref, accept_ref, lengths_ref, perm_ref, freq_ref,
    out_ref, nk_ref, nv_ref,
    wbuf, obuf_w, sbuf, hbuf, abuf, kc, vc, acc, reach_ref, cos_ref, sin_ref, qb, kb, vb,
    loc, zs0, zr0, xs0, xr0, cs0, cr0, zs1, zr1, xs1, xr1, cs1, cr1, ss, rs, as0, ar0, as1, ar1, far_ok,
):
    p = Place()
    links = Links()
    slot_own = p.x * 8 + p.zl
    local = [
        pltpu.make_async_copy(wqkv_hbm, wbuf.at[:, slot_own, p.c], loc.at[0]),
        pltpu.make_async_copy(states_hbm, sbuf.at[p.mp], loc.at[1]),
        pltpu.make_async_copy(wout_hbm, obuf_w.at[slot_own, p.c], loc.at[2]),
        pltpu.make_async_copy(ck_hbm, kc, loc.at[3]),
        pltpu.make_async_copy(cv_hbm, vc, loc.at[4]),
    ]
    for copy in local:
        copy.start()
    barrier = pltpu.get_barrier_semaphore()
    peers = p.peers()
    for device in peers:
        pl.semaphore_signal(barrier, inc=1, device_id=device, device_id_type=MESH)

    qkv = Gather(
        links, p, lambda slot, core: wbuf.at[:, slot, core],
        lambda slot, core: wbuf.at[:, pl.ds(slot, 4), core], zs0, zr0, xs0, xr0, cs0, cr0,
    )
    proj = Gather(
        links, p, lambda slot, core: obuf_w.at[slot, core],
        lambda slot, core: obuf_w.at[pl.ds(slot, 4), core], zs1, zr1, xs1, xr1, cs1, cr1,
    )
    rows = Heads(links, p, lambda slot: sbuf.at[slot], ss, rs)
    mixed = [
        Heads(links, p, lambda slot: abuf.at[slot, 0], as0, ar0),
        Heads(links, p, lambda slot: abuf.at[slot, 1], as1, ar1),
    ]

    local[0].wait()
    pl.semaphore_wait(barrier, len(peers))
    pl.semaphore_signal(far_ok, inc=1, device_id=p.middle(), device_id_type=MESH)

    qkv.to_other_group()
    qkv.to_group(0)
    qkv.to_x_and_core(0)
    local[1].wait()
    rows.to_y(0)

    tree = 64
    row_id = lax.broadcasted_iota(jnp.int32, (tree, tree), 0)
    col_id = lax.broadcasted_iota(jnp.int32, (tree, tree), 1)
    col_f = col_id.astype(F32)
    own_len = []
    for r in range(2):
        own_len.append(lengths_ref[perm_ref[p.dp * 2 + r]])
        line = parents_ref[r : r + 1, :].astype(F32)
        column = jnp.sum(jnp.where(row_id == col_id, line, 0.0), axis=1, keepdims=True)
        linked = jnp.where((column == col_f) & (row_id > 0), 1.0, 0.0)
        reach = jnp.where(row_id == col_id, 1.0, 0.0) + linked
        for _ in range(6):
            half = reach.astype(BF16)
            reach = jnp.minimum(jnp.dot(half, half, preferred_element_type=F32), 1.0)
        reach_ref[r] = reach
        depth = jnp.sum(reach, axis=1, keepdims=True) - 1.0
        position = own_len[r].astype(F32) + depth
        angle = position * freq_ref[...]
        lane = lax.broadcasted_iota(jnp.int32, (tree, HEAD_DIM), 1)
        sine = jnp.sin(angle)
        cos_ref[r] = jnp.cos(angle)
        sin_ref[r] = jnp.where(lane < HEAD_DIM // 2, -sine, sine)

    for index in (1, 2, 3):
        qkv.z_arrive(index)
        qkv.to_x_and_core(index)
    qkv.z_arrive(4)
    qkv.to_group(4)
    qkv.to_x_and_core(4)
    for index in (5, 6, 7):
        qkv.z_arrive(index)
        qkv.to_x_and_core(index)
    pl.semaphore_wait(far_ok, 1)
    rows.to_far()
    local[2].wait()
    proj.to_other_group()
    proj.to_group(0)
    for step in (1, 3, 2):
        qkv.x_arrive(step, 0)
        qkv.x_to_core(step, 0)
    rows.far_arrive()
    rows.to_y(1)
    for index in (1, 2, 3):
        proj.z_arrive(index)
    proj.z_arrive(4)
    proj.to_group(4)
    for step in (1, 3, 2):
        qkv.x_arrive(step, 1)
        qkv.x_to_core(step, 1)
    for index in (0, 1, 2, 3, 4):
        proj.to_x_and_core(index)

    rows.y_arrive(0)
    rows.y_arrive(1)
    flat, width = 128, 256
    total = jnp.zeros((flat, 1), F32)
    for m in range(8):
        total = total + jnp.sum(sbuf[m].reshape(flat, width).astype(F32), axis=1, keepdims=True)
    mean = total / 2048.0
    total = jnp.zeros((flat, 1), F32)
    for m in range(8):
        centred = sbuf[m].reshape(flat, width).astype(F32) - mean
        total = total + jnp.sum(centred * centred, axis=1, keepdims=True)
    inverse = lax.rsqrt(total / 2048.0 + EPSILON)
    for m in range(8):
        centred = sbuf[m].reshape(flat, width).astype(F32) - mean
        hbuf[:, m * width : (m + 1) * width] = (centred * inverse).astype(BF16)

    for index in (5, 6, 7):
        proj.z_arrive(index)
        proj.to_x_and_core(index)

    for step in (0, 1, 3, 2):
        qkv.core_arrive(step)
        xx = mod4(p.x - step)
        part = hbuf[:, pl.ds(pl.multiple_of(xx * 512, 512), 512)]
        for j in range(3):
            block = wbuf[j, pl.ds(xx * 8, 8)].reshape(512, width)
            product = jnp.dot(part, block, preferred_element_type=F32)
            if step == 0:
                acc[j] = product
            else:
                acc[j] = acc[j] + product

    local[3].wait()
    local[4].wait()
    scale = HEAD_DIM ** (-0.5)
    slots = lax.broadcasted_iota(jnp.int32, (tree, 384), 1)
    across = (((1,), (1,)), ((), ()))
    for head in range(2):
        lanes = slice(head * HEAD_DIM, (head + 1) * HEAD_DIM)
        for r in range(2):
            span = slice(r * tree, (r + 1) * tree)
            cosine, sine = cos_ref[r], sin_ref[r]

            def turned(j):
                value = acc[j, span, lanes]
                return (value * cosine + pltpu.roll(value, HEAD_DIM // 2, 1) * sine).astype(BF16)

            queries, keys, values = turned(0), turned(1), acc[2, span, lanes].astype(BF16)
            kb[r, :, lanes] = keys
            vb[r, :, lanes] = values
            cache = lax.dot_general(queries, kc[r, :, lanes], across, preferred_element_type=F32) * scale
            cache = jnp.where(slots < own_len[r], cache, NEG_FILL)
            nodes = lax.dot_general(queries, keys, across, preferred_element_type=F32) * scale
            nodes = jnp.where(reach_ref[r] > 0, nodes, NEG_FILL)
            peak = jnp.maximum(jnp.max(cache, axis=1, keepdims=True), jnp.max(nodes, axis=1, keepdims=True))
            cache = jnp.exp(cache - peak)
            nodes = jnp.exp(nodes - peak)
            denom = jnp.sum(cache, axis=1, keepdims=True) + jnp.sum(nodes, axis=1, keepdims=True)
            cache = (cache / denom).astype(BF16)
            nodes = (nodes / denom).astype(BF16)
            blend = jnp.dot(cache, vc[r, :, lanes], preferred_element_type=F32)
            blend = blend + jnp.dot(nodes, values, preferred_element_type=F32)
            abuf[p.mp, head, span, :] = blend.astype(BF16)
        mixed[head].to_far()
        mixed[head].to_y(0)

    for r in range(2):
        line = accept_ref[r : r + 1, :].astype(F32)
        small_row = lax.broadcasted_iota(jnp.int32, (8, 8), 0)
        small_col = lax.broadcasted_iota(jnp.int32, (8, 8), 1)
        column = jnp.sum(jnp.where(small_row == small_col, line, 0.0), axis=1, keepdims=True)
        picker = jnp.where(column == lax.broadcasted_iota(jnp.int32, (8, tree), 1).astype(F32), 1.0, 0.0).astype(BF16)
        nk_ref[r] = jnp.dot(picker, kb[r], preferred_element_type=F32).astype(BF16)
        nv_ref[r] = jnp.dot(picker, vb[r], preferred_element_type=F32).astype(BF16)

    for half in (0, 1):
        for step in (1, 3, 2):
            proj.x_arrive(step, half)
            proj.x_to_core(step, half)
    for step in (0, 1, 3, 2):
        proj.core_arrive(step)
    product = sbuf[p.mp].reshape(flat, width).astype(F32)

    def projected(m):
        both = jnp.concatenate([abuf[m, 0], abuf[m, 1]], axis=1)
        block = obuf_w[pl.ds(4 * m, 4)].reshape(256, width)
        return jnp.dot(both, block, preferred_element_type=F32)

    for head in range(2):
        mixed[head].y_arrive(0)
    for step in (0, 1, 3, 2):
        product = product + projected(mod4(p.y - step) * 2 + p.zh)
    for head in range(2):
        mixed[head].far_arrive()
        mixed[head].to_y(1)
    product = product + projected(p.y * 2 + 1 - p.zh)
    for head in range(2):
        mixed[head].y_arrive(1)
    for step in (1, 3, 2):
        product = product + projected(mod4(p.y - step) * 2 + 1 - p.zh)
    out_ref[...] = product.astype(BF16).reshape(2, tree, width)
    links.drain()


def hand_out(out_in, nk_in, nv_in, out_ref, nk_ref, nv_ref):
    out_ref[...] = out_in[...]
    nk_ref[...] = nk_in[...]
    nv_ref[...] = nv_in[...]


def local(states, w_qkv, w_out, cache_keys, cache_values, parents, accept, lengths, perm):
    half = HEAD_DIM // 2
    freqs = ROPE_BASE ** (-(np.arange(half, dtype=np.float32) * np.float32(2.0) / np.float32(HEAD_DIM)))
    freqs = np.concatenate([freqs, freqs]).astype(np.float32)[None, :]
    hbm = pl.BlockSpec(memory_space=pl.ANY)
    vmem = pl.BlockSpec(memory_space=pltpu.VMEM)
    smem = pl.BlockSpec(memory_space=pltpu.SMEM)
    dma = pltpu.SemaphoreType.DMA
    gather_sems = [dma((8,)), dma((8,)), dma((8, 4)), dma((8, 4)), dma((14,)), dma((14,))]
    shapes = (
        jax.ShapeDtypeStruct((2, 64, 256), BF16),
        jax.ShapeDtypeStruct((2, 8, 256), BF16),
        jax.ShapeDtypeStruct((2, 8, 256), BF16),
    )
    results = pl.pallas_call(
        kernel,
        name="sublayer",
        out_shape=shapes,
        in_specs=[hbm, hbm, hbm, hbm, hbm, vmem, vmem, smem, smem, vmem],
        out_specs=(vmem, vmem, vmem),
        scratch_shapes=[
            pltpu.VMEM((3, 32, 2, 32, 256), BF16),
            pltpu.VMEM((32, 2, 32, 256), BF16),
            pltpu.VMEM((8, 2, 64, 256), BF16),
            pltpu.VMEM((128, 2048), BF16),
            pltpu.VMEM((8, 2, 128, 128), BF16),
            pltpu.VMEM((2, 384, 256), BF16),
            pltpu.VMEM((2, 384, 256), BF16),
            pltpu.VMEM((3, 128, 256), F32),
            pltpu.VMEM((2, 64, 64), F32),
            pltpu.VMEM((2, 64, 128), F32),
            pltpu.VMEM((2, 64, 128), F32),
            pltpu.VMEM((2, 64, 256), BF16),
            pltpu.VMEM((2, 64, 256), BF16),
            pltpu.VMEM((2, 64, 256), BF16),
            dma((5,)), *gather_sems, *gather_sems,
            dma((8,)), dma((8,)), dma((8,)), dma((8,)), dma((8,)), dma((8,)), pltpu.SemaphoreType.REGULAR,
        ],
        compiler_params=pltpu.CompilerParams(collective_id=0, has_side_effects=True),
    )(states, w_qkv, w_out, cache_keys, cache_values, parents, accept, lengths, perm, jnp.asarray(freqs))
    return pl.pallas_call(hand_out, name="hand_out", out_shape=shapes, in_specs=[vmem] * 3, out_specs=(vmem,) * 3)(*results)


def solution(mesh):
    in_specs = (
        P("dp", None, "mp"),
        P(None, "dp", "mp"),
        P("dp", "mp"),
        P("dp", None, "mp"),
        P("dp", None, "mp"),
        P("dp", None),
        P("dp", None),
        P(),
        P(),
    )
    out_specs = (P("dp", None, "mp"), P("dp", None, "mp"), P("dp", None, "mp"))
    return jax.shard_map(local, mesh=mesh, in_specs=in_specs, out_specs=out_specs, check_vma=False)
```

```python
import functools

import jax
import jax.numpy as jnp
import numpy as np
from jax import lax
from jax.experimental import pallas as pl
from jax.experimental.pallas import tpu as pltpu
from jax.sharding import PartitionSpec as P

HEAD_DIM = 128
EPSILON = 1e-05
ROPE_BASE = 10000.0
NEG_FILL = -1e30
MESH = pl.DeviceIdType.MESH
F32 = jnp.float32
BF16 = jnp.bfloat16


def mod4(value):
    return lax.rem(value + 8, 4)


class Links:
    def __init__(self):
        self.started = []

    def send(self, view, send_sem, recv_sem, device, source=None):
        copy = pltpu.make_async_remote_copy(
            src_ref=view if source is None else source, dst_ref=view, send_sem=send_sem, recv_sem=recv_sem,
            device_id=device, device_id_type=MESH,
        )
        copy.start()
        self.started.append(copy)

    def arrive(self, view, send_sem, recv_sem, device):
        pltpu.make_async_remote_copy(
            src_ref=view, dst_ref=view, send_sem=send_sem, recv_sem=recv_sem,
            device_id=device, device_id_type=MESH,
        ).wait_recv()

    def drain(self):
        for copy in self.started:
            copy.wait_send()


class Gather:
    def __init__(self, links, place, own, shard, batch, zs, zr, xs, xr, cs, cr):
        self.own = own
        self.links, self.place, self.shard, self.batch = links, place, shard, batch
        self.zs, self.zr, self.xs, self.xr, self.cs, self.cr = zs, zr, xs, xr, cs, cr

    def z_source(self, index):
        p = self.place
        group = p.g if index < 4 else 1 - p.g
        return group * 4 + mod4(p.q - index % 4)

    def x_source(self, step):
        return mod4(self.place.x - step)

    def view(self, index, step, core):
        return self.shard(self.x_source(step) * 8 + self.z_source(index), core)

    def source(self, index):
        return self.own if index == 0 else None

    def to_group(self, base):
        p = self.place
        for k in (1, 2, 3):
            device = p.at(zl=p.g * 4 + mod4(p.q + k))
            self.links.send(self.view(base, 0, p.c), self.zs.at[base + k], self.zr.at[base + k], device, self.source(base))

    def to_other_group(self):
        p = self.place
        self.links.send(self.view(0, 0, p.c), self.zs.at[4], self.zr.at[4], p.at(zl=(1 - p.g) * 4 + p.q), self.own)

    def to_x_and_core(self, index):
        p = self.place
        for step in (2, 1, 3):
            self.links.send(
                self.view(index, 0, p.c), self.xs.at[index, step], self.xr.at[index, step], p.at(x=mod4(p.x + step)),
                self.source(index),
            )
        self.links.send(self.view(index, 0, p.c), self.cs.at[index], self.cr.at[index], p.at(c=1 - p.c), self.source(index))

    def z_arrive(self, index):
        p = self.place
        self.links.arrive(self.view(index, 0, p.c), self.zs.at[index], self.zr.at[index], p.at(c=1 - p.c))

    def x_arrive(self, step, half):
        p = self.place
        for index in range(4 * half, 4 * half + 4):
            self.links.arrive(
                self.view(index, step, p.c), self.xs.at[index, step], self.xr.at[index, step], p.at(c=1 - p.c)
            )

    def group_view(self, step, half, core):
        group = self.place.g if half == 0 else 1 - self.place.g
        return self.batch(self.x_source(step) * 8 + group * 4, core)

    def x_to_core(self, step, half):
        p = self.place
        slot = 8 + (step - 1) * 2 + half
        self.links.send(self.group_view(step, half, p.c), self.cs.at[slot], self.cr.at[slot], p.at(c=1 - p.c))

    def core_arrive(self, step):
        p = self.place
        if step == 0:
            for index in range(8):
                self.links.arrive(self.view(index, 0, 1 - p.c), self.cs.at[index], self.cr.at[index], p.at(c=1 - p.c))
        else:
            for half in (0, 1):
                slot = 8 + (step - 1) * 2 + half
                self.links.arrive(
                    self.group_view(step, half, 1 - p.c), self.cs.at[slot], self.cr.at[slot], p.at(c=1 - p.c)
                )


class Heads:
    def __init__(self, links, place, piece, ss, rs):
        self.links, self.place, self.piece, self.ss, self.rs = links, place, piece, ss, rs

    def to_y(self, far):
        p = self.place
        slot = p.y * 2 + (1 - p.zh if far else p.zh)
        for step in (2, 1, 3):
            index = far * 4 + step
            self.links.send(self.piece(slot), self.ss.at[index], self.rs.at[index], p.at(y=mod4(p.y + step)))

    def to_far(self):
        p = self.place
        self.links.send(self.piece(p.y * 2 + p.zh), self.ss.at[0], self.rs.at[0], p.at(zh=1 - p.zh))

    def far_arrive(self):
        p = self.place
        self.links.arrive(self.piece(p.y * 2 + 1 - p.zh), self.ss.at[0], self.rs.at[0], p.at(zh=1 - p.zh))

    def y_arrive(self, far):
        p = self.place
        for step in (1, 3, 2):
            index = far * 4 + step
            slot = mod4(p.y - step) * 2 + (1 - p.zh if far else p.zh)
            self.links.arrive(self.piece(slot), self.ss.at[index], self.rs.at[index], p.at(c=1 - p.c))


class Place:
    def __init__(self):
        dp, mp = lax.axis_index("dp"), lax.axis_index("mp")
        self.dp, self.mp = dp, mp
        self.x, self.zl, self.c = lax.div(dp, 16), lax.rem(lax.div(dp, 2), 8), lax.rem(dp, 2)
        self.g, self.q = lax.div(self.zl, 4), lax.rem(self.zl, 4)
        self.y, self.zh = lax.div(mp, 2), lax.rem(mp, 2)

    def at(self, x=None, zl=None, c=None, y=None, zh=None):
        x = self.x if x is None else x
        zl = self.zl if zl is None else zl
        c = self.c if c is None else c
        y = self.y if y is None else y
        zh = self.zh if zh is None else zh
        return (x * 16 + zl * 2 + c, y * 2 + zh)

    def middle(self):
        return self.at(zl=(1 - self.g) * 4 + self.q, zh=1 - self.zh)

    def peers(self):
        found = [self.at(c=1 - self.c)]
        found += [self.at(x=mod4(self.x + k)) for k in (1, 2, 3)]
        found += [self.at(y=mod4(self.y + k)) for k in (1, 2, 3)]
        found += [self.at(zl=self.g * 4 + mod4(self.q + k)) for k in (1, 2, 3)]
        found += [self.at(zl=(1 - self.g) * 4 + self.q), self.middle()]
        return found


def kernel(
    states_hbm, wqkv_hbm, wout_hbm, ck_hbm, cv_hbm, parents_ref, accept_ref, lengths_ref, perm_ref, freq_ref,
    out_ref, nk_ref, nv_ref,
    wbuf, obuf_w, sbuf, hbuf, abuf, kc, vc, acc, reach_ref, cos_ref, sin_ref, qb, kb, vb,
    loc, zs0, zr0, xs0, xr0, cs0, cr0, zs1, zr1, xs1, xr1, cs1, cr1, ss, rs, as0, ar0, as1, ar1, far_ok,
):
    p = Place()
    links = Links()
    slot_own = p.x * 8 + p.zl
    local = [
        pltpu.make_async_copy(wqkv_hbm, wbuf.at[:, slot_own, p.c], loc.at[0]),
        pltpu.make_async_copy(states_hbm, sbuf.at[p.mp], loc.at[1]),
        pltpu.make_async_copy(wout_hbm, obuf_w.at[slot_own, p.c], loc.at[2]),
        pltpu.make_async_copy(ck_hbm, kc, loc.at[3]),
        pltpu.make_async_copy(cv_hbm, vc, loc.at[4]),
    ]
    for copy in local:
        copy.start()
    barrier = pltpu.get_barrier_semaphore()
    peers = p.peers()
    for device in peers:
        pl.semaphore_signal(barrier, inc=1, device_id=device, device_id_type=MESH)

    qkv = Gather(
        links, p, wqkv_hbm, lambda slot, core: wbuf.at[:, slot, core],
        lambda slot, core: wbuf.at[:, pl.ds(slot, 4), core], zs0, zr0, xs0, xr0, cs0, cr0,
    )
    proj = Gather(
        links, p, wout_hbm, lambda slot, core: obuf_w.at[slot, core],
        lambda slot, core: obuf_w.at[pl.ds(slot, 4), core], zs1, zr1, xs1, xr1, cs1, cr1,
    )
    rows = Heads(links, p, lambda slot: sbuf.at[slot], ss, rs)
    mixed = [
        Heads(links, p, lambda slot: abuf.at[slot, 0], as0, ar0),
        Heads(links, p, lambda slot: abuf.at[slot, 1], as1, ar1),
    ]

    pl.semaphore_wait(barrier, len(peers))
    pl.semaphore_signal(far_ok, inc=1, device_id=p.middle(), device_id_type=MESH)

    qkv.to_other_group()
    qkv.to_group(0)
    qkv.to_x_and_core(0)
    local[1].wait()
    rows.to_y(0)

    tree = 64
    row_id = lax.broadcasted_iota(jnp.int32, (tree, tree), 0)
    col_id = lax.broadcasted_iota(jnp.int32, (tree, tree), 1)
    col_f = col_id.astype(F32)
    own_len = []
    for r in range(2):
        own_len.append(lengths_ref[perm_ref[p.dp * 2 + r]])
        line = parents_ref[r : r + 1, :].astype(F32)
        column = jnp.sum(jnp.where(row_id == col_id, line, 0.0), axis=1, keepdims=True)
        linked = jnp.where((column == col_f) & (row_id > 0), 1.0, 0.0)
        reach = jnp.where(row_id == col_id, 1.0, 0.0) + linked
        for _ in range(6):
            half = reach.astype(BF16)
            reach = jnp.minimum(jnp.dot(half, half, preferred_element_type=F32), 1.0)
        reach_ref[r] = reach
        depth = jnp.sum(reach, axis=1, keepdims=True) - 1.0
        position = own_len[r].astype(F32) + depth
        angle = position * freq_ref[...]
        lane = lax.broadcasted_iota(jnp.int32, (tree, HEAD_DIM), 1)
        sine = jnp.sin(angle)
        cos_ref[r] = jnp.cos(angle)
        sin_ref[r] = jnp.where(lane < HEAD_DIM // 2, -sine, sine)

    for index in (1, 2, 3):
        qkv.z_arrive(index)
        qkv.to_x_and_core(index)
    qkv.z_arrive(4)
    qkv.to_group(4)
    qkv.to_x_and_core(4)
    for index in (5, 6, 7):
        qkv.z_arrive(index)
        qkv.to_x_and_core(index)
    pl.semaphore_wait(far_ok, 1)
    rows.to_far()
    proj.to_other_group()
    proj.to_group(0)
    for step in (1, 3, 2):
        qkv.x_arrive(step, 0)
        qkv.x_to_core(step, 0)
    rows.far_arrive()
    rows.to_y(1)
    for index in (1, 2, 3):
        proj.z_arrive(index)
    proj.z_arrive(4)
    proj.to_group(4)
    for step in (1, 3, 2):
        qkv.x_arrive(step, 1)
        qkv.x_to_core(step, 1)
    for index in (0, 1, 2, 3, 4):
        proj.to_x_and_core(index)

    rows.y_arrive(0)
    rows.y_arrive(1)
    flat, width = 128, 256
    total = jnp.zeros((flat, 1), F32)
    for m in range(8):
        total = total + jnp.sum(sbuf[m].reshape(flat, width).astype(F32), axis=1, keepdims=True)
    mean = total / 2048.0
    total = jnp.zeros((flat, 1), F32)
    for m in range(8):
        centred = sbuf[m].reshape(flat, width).astype(F32) - mean
        total = total + jnp.sum(centred * centred, axis=1, keepdims=True)
    inverse = lax.rsqrt(total / 2048.0 + EPSILON)
    for m in range(8):
        centred = sbuf[m].reshape(flat, width).astype(F32) - mean
        hbuf[:, m * width : (m + 1) * width] = (centred * inverse).astype(BF16)

    for index in (5, 6, 7):
        proj.z_arrive(index)
        proj.to_x_and_core(index)

    local[0].wait()
    local[2].wait()
    for step in (0, 1, 3, 2):
        qkv.core_arrive(step)
        xx = mod4(p.x - step)
        part = hbuf[:, pl.ds(pl.multiple_of(xx * 512, 512), 512)]
        for j in range(3):
            block = wbuf[j, pl.ds(xx * 8, 8)].reshape(512, width)
            product = jnp.dot(part, block, preferred_element_type=F32)
            if step == 0:
                acc[j] = product
            else:
                acc[j] = acc[j] + product

    local[3].wait()
    local[4].wait()
    scale = HEAD_DIM ** (-0.5)
    slots = lax.broadcasted_iota(jnp.int32, (tree, 384), 1)
    across = (((1,), (1,)), ((), ()))
    for head in range(2):
        lanes = slice(head * HEAD_DIM, (head + 1) * HEAD_DIM)
        for r in range(2):
            span = slice(r * tree, (r + 1) * tree)
            cosine, sine = cos_ref[r], sin_ref[r]

            def turned(j):
                value = acc[j, span, lanes]
                return (value * cosine + pltpu.roll(value, HEAD_DIM // 2, 1) * sine).astype(BF16)

            queries, keys, values = turned(0), turned(1), acc[2, span, lanes].astype(BF16)
            kb[r, :, lanes] = keys
            vb[r, :, lanes] = values
            cache = lax.dot_general(queries, kc[r, :, lanes], across, preferred_element_type=F32) * scale
            cache = jnp.where(slots < own_len[r], cache, NEG_FILL)
            nodes = lax.dot_general(queries, keys, across, preferred_element_type=F32) * scale
            nodes = jnp.where(reach_ref[r] > 0, nodes, NEG_FILL)
            peak = jnp.maximum(jnp.max(cache, axis=1, keepdims=True), jnp.max(nodes, axis=1, keepdims=True))
            cache = jnp.exp(cache - peak)
            nodes = jnp.exp(nodes - peak)
            denom = jnp.sum(cache, axis=1, keepdims=True) + jnp.sum(nodes, axis=1, keepdims=True)
            cache = (cache / denom).astype(BF16)
            nodes = (nodes / denom).astype(BF16)
            blend = jnp.dot(cache, vc[r, :, lanes], preferred_element_type=F32)
            blend = blend + jnp.dot(nodes, values, preferred_element_type=F32)
            abuf[p.mp, head, span, :] = blend.astype(BF16)
        mixed[head].to_far()
        mixed[head].to_y(0)

    for r in range(2):
        line = accept_ref[r : r + 1, :].astype(F32)
        small_row = lax.broadcasted_iota(jnp.int32, (8, 8), 0)
        small_col = lax.broadcasted_iota(jnp.int32, (8, 8), 1)
        column = jnp.sum(jnp.where(small_row == small_col, line, 0.0), axis=1, keepdims=True)
        picker = jnp.where(column == lax.broadcasted_iota(jnp.int32, (8, tree), 1).astype(F32), 1.0, 0.0).astype(BF16)
        nk_ref[r] = jnp.dot(picker, kb[r], preferred_element_type=F32).astype(BF16)
        nv_ref[r] = jnp.dot(picker, vb[r], preferred_element_type=F32).astype(BF16)

    for half in (0, 1):
        for step in (1, 3, 2):
            proj.x_arrive(step, half)
            proj.x_to_core(step, half)
    for step in (0, 1, 3, 2):
        proj.core_arrive(step)
    product = sbuf[p.mp].reshape(flat, width).astype(F32)

    def projected(m):
        both = jnp.concatenate([abuf[m, 0], abuf[m, 1]], axis=1)
        block = obuf_w[pl.ds(4 * m, 4)].reshape(256, width)
        return jnp.dot(both, block, preferred_element_type=F32)

    for head in range(2):
        mixed[head].y_arrive(0)
    for step in (0, 1, 3, 2):
        product = product + projected(mod4(p.y - step) * 2 + p.zh)
    for head in range(2):
        mixed[head].far_arrive()
        mixed[head].to_y(1)
    product = product + projected(p.y * 2 + 1 - p.zh)
    for head in range(2):
        mixed[head].y_arrive(1)
    for step in (1, 3, 2):
        product = product + projected(mod4(p.y - step) * 2 + 1 - p.zh)
    out_ref[...] = product.astype(BF16).reshape(2, tree, width)
    links.drain()


def hand_out(out_in, nk_in, nv_in, out_ref, nk_ref, nv_ref):
    out_ref[...] = out_in[...]
    nk_ref[...] = nk_in[...]
    nv_ref[...] = nv_in[...]


def local(states, w_qkv, w_out, cache_keys, cache_values, parents, accept, lengths, perm):
    half = HEAD_DIM // 2
    freqs = ROPE_BASE ** (-(np.arange(half, dtype=np.float32) * np.float32(2.0) / np.float32(HEAD_DIM)))
    freqs = np.concatenate([freqs, freqs]).astype(np.float32)[None, :]
    hbm = pl.BlockSpec(memory_space=pl.ANY)
    vmem = pl.BlockSpec(memory_space=pltpu.VMEM)
    smem = pl.BlockSpec(memory_space=pltpu.SMEM)
    dma = pltpu.SemaphoreType.DMA
    gather_sems = [dma((8,)), dma((8,)), dma((8, 4)), dma((8, 4)), dma((14,)), dma((14,))]
    shapes = (
        jax.ShapeDtypeStruct((2, 64, 256), BF16),
        jax.ShapeDtypeStruct((2, 8, 256), BF16),
        jax.ShapeDtypeStruct((2, 8, 256), BF16),
    )
    results = pl.pallas_call(
        kernel,
        name="sublayer",
        out_shape=shapes,
        in_specs=[hbm, hbm, hbm, hbm, hbm, vmem, vmem, smem, smem, vmem],
        out_specs=(vmem, vmem, vmem),
        scratch_shapes=[
            pltpu.VMEM((3, 32, 2, 32, 256), BF16),
            pltpu.VMEM((32, 2, 32, 256), BF16),
            pltpu.VMEM((8, 2, 64, 256), BF16),
            pltpu.VMEM((128, 2048), BF16),
            pltpu.VMEM((8, 2, 128, 128), BF16),
            pltpu.VMEM((2, 384, 256), BF16),
            pltpu.VMEM((2, 384, 256), BF16),
            pltpu.VMEM((3, 128, 256), F32),
            pltpu.VMEM((2, 64, 64), F32),
            pltpu.VMEM((2, 64, 128), F32),
            pltpu.VMEM((2, 64, 128), F32),
            pltpu.VMEM((2, 64, 256), BF16),
            pltpu.VMEM((2, 64, 256), BF16),
            pltpu.VMEM((2, 64, 256), BF16),
            dma((5,)), *gather_sems, *gather_sems,
            dma((8,)), dma((8,)), dma((8,)), dma((8,)), dma((8,)), dma((8,)), pltpu.SemaphoreType.REGULAR,
        ],
        compiler_params=pltpu.CompilerParams(collective_id=0, has_side_effects=True),
    )(states, w_qkv, w_out, cache_keys, cache_values, parents, accept, lengths, perm, jnp.asarray(freqs))
    return pl.pallas_call(hand_out, name="hand_out", out_shape=shapes, in_specs=[vmem] * 3, out_specs=(vmem,) * 3)(*results)


def solution(mesh):
    in_specs = (
        P("dp", None, "mp"),
        P(None, "dp", "mp"),
        P("dp", "mp"),
        P("dp", None, "mp"),
        P("dp", None, "mp"),
        P("dp", None),
        P("dp", None),
        P(),
        P(),
    )
    out_specs = (P("dp", None, "mp"), P("dp", None, "mp"), P("dp", None, "mp"))
    return jax.shard_map(local, mesh=mesh, in_specs=in_specs, out_specs=out_specs, check_vma=False)
```
